32 devices in a mesh: groups: 2 (over x), band: 16 (over z, y, core).
Axes of the slice: x: 2, y: 2, z: 4, core: 2. Of those that a mesh axis runs over, the one named last changes fastest.
Arguments:
- orbitals: bfloat16 [2560, 32, 128], P(('groups', 'band')), parts along dimension 0, may hold values from -24 to 24
- potential: float32 [64, 128], P('groups'), parts along dimension 0, may hold values from -2 to 0
- plan: int32 [4, 16], P('groups'), parts along dimension 0, may hold values from 0 to 15, as said below
- owners: int32 [4, 16], P('groups'), parts along dimension 0, may hold values from 0 to 15, each once within a row
Outputs:
- filtered: bfloat16 [2560, 32, 128], P(('groups', 'band')), parts along dimension 0
- tiles: float32 [2, 2560, 80], P(None, ('groups', 'band')), parts along dimension 1
The draws below stay inside these ranges and needn't reach their ends.
There are 2 independent parts, one for each index of `groups`. The reference program is written for one: setup_inputs(seed, part) draws one part's arguments, and reference() takes and returns one part's arrays. A program takes and returns all parts, laid end to end along the dimension named above; each array names one. Nothing has to cross between parts.
Inputs may be any that keep to these rules, and one draw needn't show every extreme that they name: In each of the 2 rounds the band groups are paired by a round-robin tournament: plan[r, i] is never i and plan[r, plan[r, i]] = i. `owners`: each row is a permutation of the band groups.
All inputs are finite; a program needn't handle non-finite values.
Results may differ from the reference program's by a relative error of at most 0.0055.
Values may be sent and summed in bfloat16 or wider, within the bound.
A program may use at most 192 MiB of HBM per device.

```python
import math
import jax
import jax.numpy as jnp
from jax import lax

BAND_DEV = 80
NY = 8
NZ = 16
DEGREE = 2
ROUNDS = 2
BLOCKS = 16
NX = 32
NBANDS = 1280


def draw_plan(key, part):
    group_total = BLOCKS
    circle_size = group_total - 1
    label_key, offset_key = jax.random.split(jax.random.fold_in(key, 17))
    labels = jax.random.permutation(label_key, group_total).astype(jnp.int32)
    offset = jax.random.randint(offset_key, (), 0, circle_size).astype(jnp.int32)
    position = jnp.arange(group_total, dtype=jnp.int32)

    def one_round(round_index):
        turn_seat = (offset + round_index) % circle_size
        paired = jnp.where(position == group_total - 1, turn_seat, jnp.where(position == turn_seat, group_total - 1, (2 * turn_seat - position) % circle_size))
        return jnp.zeros((group_total,), jnp.int32).at[labels].set(labels[paired])
    return jax.vmap(one_round)(jnp.arange(ROUNDS, dtype=jnp.int32)).astype(jnp.int32)


def block_levels(rng, dims, cuts, smallest, top_value):
    level = 1.0
    for dim, parts in cuts:
        heights = jax.random.uniform(jax.random.fold_in(jax.random.fold_in(rng, 6), dim), (parts,), jnp.float32, smallest / len(cuts), top_value / len(cuts))
        level = level * jnp.repeat(jnp.exp(heights), dims[dim] // parts).reshape((-1,) + (1,) * (len(dims) - 1 - dim))
    return level


def scatter_about(rng, shape, spread, bound, shards=(), held_as=jnp.bfloat16):
    result = jax.random.normal(rng, shape, jnp.float32) * spread
    if len(shards) > 0:
        result = block_levels(rng, shape, shards, -0.22, 0.18) * result
    return jnp.clip(result, min=-bound, max=bound).astype(held_as)


def setup_inputs(seed: int = 0, part: int = 0) -> dict:
    streams_of = jax.random.split(jax.random.key(seed), 5)
    own_keys = jax.random.split(jax.random.fold_in(streams_of[4], part), 5)
    return {
        "orbitals": scatter_about(own_keys[0], (NBANDS, NX, NY * NZ), 4.0, 24.0, ((0, 16),)),
        "potential": jnp.clip(jax.random.uniform(own_keys[1], (NX, NY * NZ), jnp.float32, -2.0, 0.0), -2.0, 0.0),
        "plan": draw_plan(jax.random.fold_in(jax.random.fold_in(streams_of[4], part), 71), part),
        "owners": jax.vmap(lambda own: jax.random.permutation(own, BLOCKS))(jax.random.split(own_keys[3], ROUNDS)).reshape((ROUNDS, BLOCKS)).astype(jnp.int32),
    }


lower_edge = -2.5
cutoff_edge = 4.0
upper_edge = 8.5
half_width = (upper_edge - cutoff_edge) / 2.0
middle_point = (upper_edge + cutoff_edge) / 2.0

def chebyshev_filter(start_values, operator):
    sigma_zero = half_width / (lower_edge - middle_point)
    previous = start_values
    current = sigma_zero / half_width * (operator(start_values) - middle_point * start_values)
    sigma_now = sigma_zero
    for degree_step in range(DEGREE - 1):
        sigma_next = 1.0 / (2.0 / sigma_zero - sigma_now)
        following = 2.0 * sigma_next / half_width * (operator(current) - middle_point * current) - sigma_now * sigma_next * previous
        previous, current, sigma_now = (current, following, sigma_next)
    return current

def second_diff(values, axis_number):
    length = values.shape[axis_number]
    widths = [(0, 0)] * values.ndim
    widths[axis_number] = (2, 2)
    padded = jnp.pad(values, widths)
    near = lax.slice_in_dim(padded, 3, 3 + length, axis=axis_number) + lax.slice_in_dim(padded, 1, 1 + length, axis=axis_number)
    far_cells = lax.slice_in_dim(padded, 4, 4 + length, axis=axis_number) + lax.slice_in_dim(padded, 0, length, axis=axis_number)
    return -2.5 * values + 4.0 / 3.0 * near - 1.0 / 12.0 * far_cells

def hamiltonian(values, potential):
    grid_cube = values.reshape(values.shape[0], values.shape[1], NY, NZ)
    laplace = second_diff(grid_cube, 1) + second_diff(grid_cube, 2) + second_diff(grid_cube, 3)
    return potential * values - 0.5 * laplace.reshape(values.shape)

def reference(orbitals, potential, plan, owners):
    cell_total = NX * NY * NZ
    norm_factor = 1.0 / math.sqrt(cell_total)
    band_blocks = orbitals.reshape(BLOCKS, BAND_DEV, NX, NY * NZ)

    def filter_block(band_block):
        return chebyshev_filter(band_block.astype(jnp.float32), lambda values: hamiltonian(values, potential)).astype(jnp.bfloat16)
    filtered = lax.map(filter_block, band_blocks)

    def image_block(band_block):
        return hamiltonian(band_block.astype(jnp.float32), potential).astype(jnp.bfloat16)
    applied = lax.map(image_block, filtered)
    flat_filtered = filtered.reshape(BLOCKS, BAND_DEV, cell_total)
    flat_applied = applied.reshape(BLOCKS, BAND_DEV, cell_total)

    def group_tiles(group_index):
        own_block = lax.dynamic_index_in_dim(flat_filtered, group_index, 0, keepdims=False)
        collected = []
        for round_index in range(ROUNDS):
            partner = plan[round_index, group_index].astype(jnp.int32)
            theirs = lax.dynamic_index_in_dim(flat_applied, partner, 0, keepdims=False)
            collected.append(jnp.dot(own_block, theirs.T, preferred_element_type=jnp.float32) * norm_factor)
        return jnp.stack(collected)
    all_tiles = lax.map(group_tiles, jnp.arange(BLOCKS, dtype=jnp.int32))
    ordered = []
    for round_index in range(ROUNDS):
        inverse = jnp.argsort(owners[round_index]).astype(jnp.int32)
        ordered.append(all_tiles[inverse, round_index].reshape(BLOCKS * BAND_DEV, BAND_DEV))
    return (filtered.reshape(NBANDS, NX, NY * NZ), jnp.stack(ordered))
```

```python
import functools
import math

import jax
import jax.numpy as jnp
from jax import lax
from jax.experimental import pallas as pl
from jax.experimental.pallas import tpu as pltpu
from jax.sharding import PartitionSpec as P

NZ = 16
ROUNDS = 2
CHUNK = 16
BLOCK = 8

lower_edge = -2.5
cutoff_edge = 4.0
upper_edge = 8.5
half_width = (upper_edge - cutoff_edge) / 2.0
middle_point = (upper_edge + cutoff_edge) / 2.0
sigma_zero = half_width / (lower_edge - middle_point)
sigma_next = 1.0 / (2.0 / sigma_zero - sigma_zero)
first_scale = sigma_zero / half_width
second_scale = 2.0 * sigma_next / half_width
back_scale = sigma_zero * sigma_next


def plane_matrix():
    row = lax.broadcasted_iota(jnp.int32, (128, 128), 0)
    col = lax.broadcasted_iota(jnp.int32, (128, 128), 1)
    gap = jnp.abs(row - col)
    same = (row // NZ) == (col // NZ)
    near = (same & (gap == 1)) | (gap == NZ)
    far = (same & (gap == 2)) | (gap == 2 * NZ)
    return jnp.where(
        gap == 0, -90.0, jnp.where(near, 16.0, jnp.where(far, -1.0, 0.0))
    ).astype(jnp.bfloat16)


def body(
    n, orb, pot, plan, owners, filt, tiles,
    wide, y0, y1, fil, matrix, send, recv, part, gathered, inverse,
    send_sem, recv_sem, relay_send, relay_recv, part_send, part_recv,
):
    me = lax.axis_index("band")
    core = lax.rem(me, 2)
    chip = me // 2
    chips = n // 2
    other = me + 1 - 2 * core
    bands, nx = orb.shape[0], orb.shape[1]
    chunks = bands // CHUNK
    planes = nx // n
    norm = 1.0 / math.sqrt(nx * orb.shape[2])

    barrier = pltpu.get_barrier_semaphore()

    def greet(o, c):
        pl.semaphore_signal(barrier, inc=1, device_id={"band": lax.rem(me + o, n)})
        return c

    lax.fori_loop(1, n, greet, 0)

    def walk(_, c):
        a, b, am, bm = c
        a = plan[1, plan[0, a]]
        b = plan[1, plan[0, b]]
        return a, b, jnp.minimum(am, a), jnp.minimum(bm, b)

    b0 = plan[0, me]
    _, _, am, bm = lax.fori_loop(0, n // 2, walk, (me, b0, me, b0))
    plain = am < bm

    matrix[...] = plane_matrix()
    edge = jnp.zeros((2, CHUNK, 128), jnp.float32)
    for buf in (y0, y1, fil):
        buf[0:2] = edge
        buf[nx + 2 : nx + 4] = edge

    def lap(buf, start, split):
        v = buf[pl.ds(start, BLOCK + 4)]
        mid = v[2 : 2 + BLOCK].reshape(BLOCK * CHUNK, 128)
        high = mid.astype(jnp.bfloat16)
        m = matrix[...]
        out = jnp.dot(high, m, preferred_element_type=jnp.float32)
        if split:
            low = (mid - high.astype(jnp.float32)).astype(jnp.bfloat16)
            out = out + jnp.dot(low, m, preferred_element_type=jnp.float32)
        out = out.reshape(BLOCK, CHUNK, 128)
        out = out + 16.0 * (v[1 : 1 + BLOCK] + v[3 : 3 + BLOCK])
        out = out - (v[0:BLOCK] + v[4 : 4 + BLOCK])
        return v[2 : 2 + BLOCK], out * (1.0 / 24.0)

    def local_pot(start):
        return pot[pl.ds(start, BLOCK), :].reshape(BLOCK, 1, 128)

    blocks = nx // BLOCK

    def each_block(fn):
        if blocks <= 4:
            for b in range(blocks):
                fn(b * BLOCK)
        else:
            def step(b, c):
                fn(pl.multiple_of(b * BLOCK, BLOCK))
                return c

            lax.fori_loop(0, blocks, step, 0)

    def one_chunk(ch, c):
        base = pl.multiple_of(ch * CHUNK, CHUNK)
        wide[...] = orb[pl.ds(base, CHUNK)].astype(jnp.float32).reshape(CHUNK * nx, 128)

        def take(start):
            for j in range(BLOCK):
                y0[start + 2 + j] = wide[pl.ds(start + j, CHUNK, stride=nx), :]

        each_block(take)

        def first(start):
            v, l = lap(y0, start, False)
            y1[pl.ds(start + 2, BLOCK)] = first_scale * ((local_pot(start) - middle_point) * v - l)

        each_block(first)

        def second(start):
            v, l = lap(y1, start, True)
            f = second_scale * ((local_pot(start) - middle_point) * v - l) - back_scale * y0[
                pl.ds(start + 2, BLOCK)
            ]
            f = f.astype(jnp.bfloat16).astype(jnp.float32)
            fil[pl.ds(start + 2, BLOCK)] = f
            for j in range(BLOCK):
                wide[pl.ds(start + j, CHUNK, stride=nx), :] = f[j]

        each_block(second)
        filt[pl.ds(base, CHUNK)] = wide[...].reshape(CHUNK, nx, 128).astype(jnp.bfloat16)

        def third(start):
            v, l = lap(fil, start, False)
            x = jnp.where(plain, v, local_pot(start) * v - l).astype(jnp.bfloat16)
            for q in range(BLOCK // planes):
                for j in range(planes):
                    send[ch, start // planes + q, :, j * 128 : (j + 1) * 128] = x[q * planes + j]

        each_block(third)

        @pl.when(ch == 0)
        def _():
            pl.semaphore_wait(barrier, n - 1)

        def push(o, c):
            d = lax.rem(me + o, n)
            pltpu.make_async_remote_copy(
                src_ref=send.at[ch, d],
                dst_ref=recv.at[lax.rem(d, 2), ch, me],
                send_sem=send_sem.at[ch],
                recv_sem=recv_sem.at[ch],
                device_id={"band": d},
            ).start()
            return c

        lax.fori_loop(1, n, push, 0)
        recv[core, ch, me] = send[ch, me]
        return c

    lax.fori_loop(0, chunks, one_chunk, 0)

    for r in range(ROUNDS):
        def find(j, c, r=r):
            d = 2 * j + core

            def look(i, found):
                return jnp.where(owners[r, i] == d, i, found)

            inverse[r, j] = lax.fori_loop(0, n, look, jnp.int32(0), unroll=8)
            return c

        lax.fori_loop(0, chips, find, 0)

    def all_but_one(ch):
        return pltpu.make_async_remote_copy(
            src_ref=send.at[ch, 0 : n - 1],
            dst_ref=recv.at[core, ch, 0 : n - 1],
            send_sem=send_sem.at[ch],
            recv_sem=recv_sem.at[ch],
            device_id={"band": other},
        )

    def relay(ch):
        return pltpu.make_async_remote_copy(
            src_ref=recv.at[core, ch],
            dst_ref=recv.at[core, ch],
            send_sem=relay_send.at[ch],
            recv_sem=relay_recv.at[ch],
            device_id={"band": other},
        )

    for ch in range(chunks):
        all_but_one(ch).wait_recv()
        relay(ch).start()
    for ch in range(chunks):
        pltpu.make_async_remote_copy(
            src_ref=recv.at[core, ch],
            dst_ref=recv.at[1 - core, ch],
            send_sem=relay_send.at[ch],
            recv_sem=relay_recv.at[ch],
            device_id={"band": other},
        ).wait_recv()

    def tile(r, j):
        i = inverse[r, j]
        p = plan[r, i]
        total = jnp.zeros((bands, bands), jnp.float32)
        for half in range(2):
            left = recv[half, :, i].reshape(bands, planes * 128)
            right = recv[half, :, p].reshape(bands, planes * 128)
            total = total + lax.dot_general(
                left, right, (((1,), (1,)), ((), ())), preferred_element_type=jnp.float32
            )
        return total * norm

    def produce(o, c):
        j = lax.rem(chip + o, chips)
        for r in range(ROUNDS):
            part[j, r] = tile(r, j).astype(jnp.bfloat16)
        pltpu.make_async_remote_copy(
            src_ref=part.at[j],
            dst_ref=gathered.at[chip],
            send_sem=part_send,
            recv_sem=part_recv,
            device_id={"band": 2 * j + core},
        ).start()
        return c

    lax.fori_loop(1, chips, produce, 0)
    for r in range(ROUNDS):
        tiles[r] = tile(r, chip)
    gathered[chip] = jnp.zeros((ROUNDS, bands, bands), jnp.bfloat16)
    last = pltpu.make_async_remote_copy(
        src_ref=part.at[0 : chips - 1],
        dst_ref=gathered.at[0 : chips - 1],
        send_sem=part_send,
        recv_sem=part_recv,
        device_id={"band": other},
    )
    last.wait_recv()

    def add(s, c):
        for r in range(ROUNDS):
            tiles[r] += gathered[s, r].astype(jnp.float32)
        return c

    lax.fori_loop(0, chips, add, 0)

    last.wait_send()
    for ch in range(chunks):
        all_but_one(ch).wait_send()
        relay(ch).wait_send()


def on_device(orbitals, potential, plan, owners):
    n = lax.axis_size("band")
    bands, nx, cells = orbitals.shape
    chunks, planes = bands // CHUNK, nx // n
    vmem = pl.BlockSpec(memory_space=pltpu.VMEM)
    smem = pl.BlockSpec(memory_space=pltpu.SMEM)
    dma = pltpu.SemaphoreType.DMA
    return pl.pallas_call(
        functools.partial(body, n),
        out_shape=(
            jax.ShapeDtypeStruct((bands, nx, cells), jnp.bfloat16),
            jax.ShapeDtypeStruct((ROUNDS, bands, bands), jnp.float32),
        ),
        in_specs=[vmem, vmem, smem, smem],
        out_specs=(vmem, vmem),
        scratch_shapes=[
            pltpu.VMEM((CHUNK * nx, 128), jnp.float32),
            pltpu.VMEM((nx + 4, CHUNK, 128), jnp.float32),
            pltpu.VMEM((nx + 4, CHUNK, 128), jnp.float32),
            pltpu.VMEM((nx + 4, CHUNK, 128), jnp.float32),
            pltpu.VMEM((128, 128), jnp.bfloat16),
            pltpu.VMEM((chunks, n, CHUNK, planes * 128), jnp.bfloat16),
            pltpu.VMEM((2, chunks, n, CHUNK, planes * 128), jnp.bfloat16),
            pltpu.VMEM((n // 2, ROUNDS, bands, bands), jnp.bfloat16),
            pltpu.VMEM((n // 2, ROUNDS, bands, bands), jnp.bfloat16),
            pltpu.SMEM((ROUNDS, n // 2), jnp.int32),
            dma((chunks,)),
            dma((chunks,)),
            dma((chunks,)),
            dma((chunks,)),
            dma,
            dma,
        ],
        compiler_params=pltpu.CompilerParams(collective_id=0, has_side_effects=True),
    )(orbitals, potential, plan, owners)


def solution(mesh):
    placed = (
        P(("groups", "band"), None, None),
        P("groups", None),
        P("groups", None),
        P("groups", None),
    )
    return jax.shard_map(
        on_device,
        mesh=mesh,
        in_specs=placed,
        out_specs=(P(("groups", "band"), None, None), P(None, ("groups", "band"), None)),
        check_vma=False,
    )
```

```python
import functools
import math

import jax
import jax.numpy as jnp
from jax import lax
from jax.experimental import pallas as pl
from jax.experimental.pallas import tpu as pltpu
from jax.sharding import PartitionSpec as P

NZ = 16
ROUNDS = 2
CHUNK = 16
BLOCK = 8

lower_edge = -2.5
cutoff_edge = 4.0
upper_edge = 8.5
half_width = (upper_edge - cutoff_edge) / 2.0
middle_point = (upper_edge + cutoff_edge) / 2.0
sigma_zero = half_width / (lower_edge - middle_point)
sigma_next = 1.0 / (2.0 / sigma_zero - sigma_zero)
first_scale = sigma_zero / half_width
second_scale = 2.0 * sigma_next / half_width
back_scale = sigma_zero * sigma_next


def plane_matrix():
    row = lax.broadcasted_iota(jnp.int32, (128, 128), 0)
    col = lax.broadcasted_iota(jnp.int32, (128, 128), 1)
    gap = jnp.abs(row - col)
    same = (row // NZ) == (col // NZ)
    near = (same & (gap == 1)) | (gap == NZ)
    far = (same & (gap == 2)) | (gap == 2 * NZ)
    return jnp.where(
        gap == 0, -90.0, jnp.where(near, 16.0, jnp.where(far, -1.0, 0.0))
    ).astype(jnp.bfloat16)


def body(
    n, orb, pot, plan, owners, filt, tiles,
    wide, y0, y1, fil, matrix, send, recv, part, gathered, inverse,
    send_sem, recv_sem, relay_send, relay_recv, part_send, part_recv,
):
    me = lax.axis_index("band")
    core = lax.rem(me, 2)
    chip = me // 2
    chips = n // 2
    other = me + 1 - 2 * core
    bands, nx = orb.shape[0], orb.shape[1]
    chunks = bands // CHUNK
    planes = nx // n
    norm = 1.0 / math.sqrt(nx * orb.shape[2])

    barrier = pltpu.get_barrier_semaphore()

    def greet(o, c):
        pl.semaphore_signal(barrier, inc=1, device_id={"band": lax.rem(me + o, n)})
        return c

    lax.fori_loop(1, n, greet, 0)

    def walk(_, c):
        a, b, am, bm = c
        a = plan[1, plan[0, a]]
        b = plan[1, plan[0, b]]
        return a, b, jnp.minimum(am, a), jnp.minimum(bm, b)

    b0 = plan[0, me]
    _, _, am, bm = lax.fori_loop(0, n // 2, walk, (me, b0, me, b0))
    plain = am < bm

    matrix[...] = plane_matrix()
    edge = jnp.zeros((2, CHUNK, 128), jnp.float32)
    for buf in (y0, y1, fil):
        buf[0:2] = edge
        buf[nx + 2 : nx + 4] = edge

    def lap(buf, start, split):
        v = buf[pl.ds(start, BLOCK + 4)]
        mid = v[2 : 2 + BLOCK].reshape(BLOCK * CHUNK, 128)
        high = mid.astype(jnp.bfloat16)
        m = matrix[...]
        out = jnp.dot(high, m, preferred_element_type=jnp.float32)
        if split:
            low = (mid - high.astype(jnp.float32)).astype(jnp.bfloat16)
            out = out + jnp.dot(low, m, preferred_element_type=jnp.float32)
        out = out.reshape(BLOCK, CHUNK, 128)
        out = out + 16.0 * (v[1 : 1 + BLOCK] + v[3 : 3 + BLOCK])
        out = out - (v[0:BLOCK] + v[4 : 4 + BLOCK])
        return v[2 : 2 + BLOCK], out * (1.0 / 24.0)

    def local_pot(start):
        return pot[pl.ds(start, BLOCK), :].reshape(BLOCK, 1, 128)

    blocks = nx // BLOCK

    def each_block(fn):
        if blocks <= 4:
            for b in range(blocks):
                fn(b * BLOCK)
        else:
            def step(b, c):
                fn(pl.multiple_of(b * BLOCK, BLOCK))
                return c

            lax.fori_loop(0, blocks, step, 0)

    def one_chunk(ch, c):
        base = pl.multiple_of(ch * CHUNK, CHUNK)
        wide[...] = orb[pl.ds(base, CHUNK)].astype(jnp.float32).reshape(CHUNK * nx, 128)

        def take(start):
            for j in range(BLOCK):
                y0[start + 2 + j] = wide[pl.ds(start + j, CHUNK, stride=nx), :]

        each_block(take)

        def first(start):
            v, l = lap(y0, start, False)
            y1[pl.ds(start + 2, BLOCK)] = first_scale * ((local_pot(start) - middle_point) * v - l)

        each_block(first)

        def second(start):
            v, l = lap(y1, start, True)
            f = second_scale * ((local_pot(start) - middle_point) * v - l) - back_scale * y0[
                pl.ds(start + 2, BLOCK)
            ]
            f = f.astype(jnp.bfloat16).astype(jnp.float32)
            fil[pl.ds(start + 2, BLOCK)] = f
            for j in range(BLOCK):
                wide[pl.ds(start + j, CHUNK, stride=nx), :] = f[j]

        each_block(second)
        filt[pl.ds(base, CHUNK)] = wide[...].reshape(CHUNK, nx, 128).astype(jnp.bfloat16)

        def third(start):
            v, l = lap(fil, start, False)
            x = jnp.where(plain, v, local_pot(start) * v - l).astype(jnp.bfloat16)
            for q in range(BLOCK // planes):
                for j in range(planes):
                    send[ch, start // planes + q, :, j * 128 : (j + 1) * 128] = x[q * planes + j]

        each_block(third)

        @pl.when(ch == 0)
        def _():
            pl.semaphore_wait(barrier, n - 1)

        def push(o, c):
            d = lax.rem(me + o, n)
            pltpu.make_async_remote_copy(
                src_ref=send.at[ch, d],
                dst_ref=recv.at[lax.rem(d, 2), ch, me],
                send_sem=send_sem.at[ch],
                recv_sem=recv_sem.at[ch],
                device_id={"band": d},
            ).start()
            return c

        lax.fori_loop(1, n, push, 0)
        recv[core, ch, me] = send[ch, me]
        return c

    lax.fori_loop(0, chunks, one_chunk, 0)

    for r in range(ROUNDS):
        def find(j, c, r=r):
            d = 2 * j + core

            def look(i, found):
                return jnp.where(owners[r, i] == d, i, found)

            inverse[r, j] = lax.fori_loop(0, n, look, jnp.int32(0), unroll=8)
            return c

        lax.fori_loop(0, chips, find, 0)

    def all_but_one(ch):
        return pltpu.make_async_remote_copy(
            src_ref=send.at[ch, 0 : n - 1],
            dst_ref=recv.at[core, ch, 0 : n - 1],
            send_sem=send_sem.at[ch],
            recv_sem=recv_sem.at[ch],
            device_id={"band": other},
        )

    def relay(ch):
        return pltpu.make_async_remote_copy(
            src_ref=recv.at[core, ch],
            dst_ref=recv.at[core, ch],
            send_sem=relay_send.at[ch],
            recv_sem=relay_recv.at[ch],
            device_id={"band": other},
        )

    for ch in range(chunks):
        all_but_one(ch).wait_recv()
        relay(ch).start()
    for ch in range(chunks):
        pltpu.make_async_remote_copy(
            src_ref=recv.at[core, ch],
            dst_ref=recv.at[1 - core, ch],
            send_sem=relay_send.at[ch],
            recv_sem=relay_recv.at[ch],
            device_id={"band": other},
        ).wait_recv()

    lead = 128 - bands
    tail = bands - lead
    strips = -(-bands // tail)
    lanes = lax.broadcasted_iota(jnp.int32, (bands, 128), 1)
    tail_lanes = lax.broadcasted_iota(jnp.int32, (tail, 128), 1)

    def product(r, j):
        i = inverse[r, j]
        p = plan[r, i]
        blank = jnp.zeros((lead, planes * 128), jnp.bfloat16)
        total = None
        for half in range(2):
            left = recv[half, :, i].reshape(bands, planes * 128)
            right = recv[half, :, p].reshape(bands, planes * 128)
            if r == 0:
                right = jnp.concatenate([right, blank], axis=0)
            else:
                right = jnp.concatenate([right[lead:], blank, right[:lead]], axis=0)
            term = lax.dot_general(
                left, right, (((1,), (1,)), ((), ())), preferred_element_type=jnp.float32
            )
            total = term if total is None else total + term
        return total * norm

    def packed(j):
        one, two = product(0, j), product(1, j)
        top = jnp.where(lanes < bands, one, two)
        low = jnp.zeros((tail, 128), jnp.float32)
        for q in range(strips):
            rows = two[q * tail : min(bands, (q + 1) * tail)]
            if rows.shape[0] < tail:
                rows = jnp.concatenate(
                    [rows, jnp.zeros((tail - rows.shape[0], 128), jnp.float32)], axis=0
                )
            if q > 0:
                rows = pltpu.roll(rows, q * tail, 1)
            here = (tail_lanes >= q * tail) & (tail_lanes < (q + 1) * tail)
            low = jnp.where(here, rows, low)
        return top, low

    def produce(o, c):
        j = lax.rem(chip + o, chips)
        top, low = packed(j)
        part[j, 0:bands] = top.astype(jnp.bfloat16)
        part[j, bands : bands + tail] = low.astype(jnp.bfloat16)
        pltpu.make_async_remote_copy(
            src_ref=part.at[j],
            dst_ref=gathered.at[chip],
            send_sem=part_send,
            recv_sem=part_recv,
            device_id={"band": 2 * j + core},
        ).start()
        return c

    lax.fori_loop(chips // 2, chips, produce, 0)
    lax.fori_loop(1, chips // 2, produce, 0)
    top, low = packed(chip)
    gathered[chip] = jnp.zeros((bands + tail, 128), jnp.bfloat16)
    last = pltpu.make_async_remote_copy(
        src_ref=part.at[0 : chips - 1],
        dst_ref=gathered.at[0 : chips - 1],
        send_sem=part_send,
        recv_sem=part_recv,
        device_id={"band": other},
    )
    last.wait_recv()
    if chips <= 8:
        for s in range(chips):
            top = top + gathered[s, 0:bands].astype(jnp.float32)
            low = low + gathered[s, bands : bands + tail].astype(jnp.float32)
    else:
        def add(s, c):
            return (
                c[0] + gathered[s, 0:bands].astype(jnp.float32),
                c[1] + gathered[s, bands : bands + tail].astype(jnp.float32),
            )

        top, low = lax.fori_loop(0, chips, add, (top, low))
    tiles[0] = top[:, 0:bands]
    front = pltpu.roll(top, lead, 1)
    backs = []
    for q in range(strips):
        rows = pltpu.roll(low, (lead - q * tail) % 128, 1) if lead != q * tail else low
        backs.append(rows[0 : min(tail, bands - q * tail)])
    back = jnp.concatenate(backs, axis=0)
    tiles[1] = jnp.where(lanes < lead, front, back)[:, 0:bands]

    last.wait_send()
    for ch in range(chunks):
        all_but_one(ch).wait_send()
        relay(ch).wait_send()


def on_device(orbitals, potential, plan, owners):
    n = lax.axis_size("band")
    bands, nx, cells = orbitals.shape
    chunks, planes = bands // CHUNK, nx // n
    vmem = pl.BlockSpec(memory_space=pltpu.VMEM)
    smem = pl.BlockSpec(memory_space=pltpu.SMEM)
    dma = pltpu.SemaphoreType.DMA
    return pl.pallas_call(
        functools.partial(body, n),
        out_shape=(
            jax.ShapeDtypeStruct((bands, nx, cells), jnp.bfloat16),
            jax.ShapeDtypeStruct((ROUNDS, bands, bands), jnp.float32),
        ),
        in_specs=[vmem, vmem, smem, smem],
        out_specs=(vmem, vmem),
        scratch_shapes=[
            pltpu.VMEM((CHUNK * nx, 128), jnp.float32),
            pltpu.VMEM((nx + 4, CHUNK, 128), jnp.float32),
            pltpu.VMEM((nx + 4, CHUNK, 128), jnp.float32),
            pltpu.VMEM((nx + 4, CHUNK, 128), jnp.float32),
            pltpu.VMEM((128, 128), jnp.bfloat16),
            pltpu.VMEM((chunks, n, CHUNK, planes * 128), jnp.bfloat16),
            pltpu.VMEM((2, chunks, n, CHUNK, planes * 128), jnp.bfloat16),
            pltpu.VMEM((n // 2, 2 * bands - (128 - bands), 128), jnp.bfloat16),
            pltpu.VMEM((n // 2, 2 * bands - (128 - bands), 128), jnp.bfloat16),
            pltpu.SMEM((ROUNDS, n // 2), jnp.int32),
            dma((chunks,)),
            dma((chunks,)),
            dma((chunks,)),
            dma((chunks,)),
            dma,
            dma,
        ],
        compiler_params=pltpu.CompilerParams(collective_id=0, has_side_effects=True),
    )(orbitals, potential, plan, owners)


def solution(mesh):
    placed = (
        P(("groups", "band"), None, None),
        P("groups", None),
        P("groups", None),
        P("groups", None),
    )
    return jax.shard_map(
        on_device,
        mesh=mesh,
        in_specs=placed,
        out_specs=(P(("groups", "band"), None, None), P(None, ("groups", "band"), None)),
        check_vma=False,
    )
```

```python
import functools
import math

import jax
import jax.numpy as jnp
from jax import lax
from jax.experimental import pallas as pl
from jax.experimental.pallas import tpu as pltpu
from jax.sharding import PartitionSpec as P

NZ = 16
ROUNDS = 2
CHUNK = 16
BLOCK = 8

lower_edge = -2.5
cutoff_edge = 4.0
upper_edge = 8.5
half_width = (upper_edge - cutoff_edge) / 2.0
middle_point = (upper_edge + cutoff_edge) / 2.0
sigma_zero = half_width / (lower_edge - middle_point)
sigma_next = 1.0 / (2.0 / sigma_zero - sigma_zero)
first_scale = sigma_zero / half_width
second_scale = 2.0 * sigma_next / half_width
back_scale = sigma_zero * sigma_next


def plane_matrix():
    row = lax.broadcasted_iota(jnp.int32, (128, 128), 0)
    col = lax.broadcasted_iota(jnp.int32, (128, 128), 1)
    gap = jnp.abs(row - col)
    same = (row // NZ) == (col // NZ)
    near = (same & (gap == 1)) | (gap == NZ)
    far = (same & (gap == 2)) | (gap == 2 * NZ)
    return jnp.where(
        gap == 0, -90.0, jnp.where(near, 16.0, jnp.where(far, -1.0, 0.0))
    ).astype(jnp.bfloat16)


def body(
    n, orb, pot, plan, owners, filt, tiles,
    wide, y0, y1, fil, matrix, send, recv, part, gathered, inverse,
    send_sem, recv_sem, relay_send, relay_recv, part_send, part_recv,
):
    me = lax.axis_index("band")
    core = lax.rem(me, 2)
    chip = me // 2
    chips = n // 2
    other = me + 1 - 2 * core
    bands, nx = orb.shape[0], orb.shape[1]
    chunks = bands // CHUNK
    planes = nx // n
    norm = 1.0 / math.sqrt(nx * orb.shape[2])

    barrier = pltpu.get_barrier_semaphore()

    def greet(o, c):
        pl.semaphore_signal(barrier, inc=1, device_id={"band": lax.rem(me + o, n)})
        return c

    lax.fori_loop(1, n, greet, 0)

    def walk(_, c):
        a, b, am, bm = c
        a = plan[1, plan[0, a]]
        b = plan[1, plan[0, b]]
        return a, b, jnp.minimum(am, a), jnp.minimum(bm, b)

    b0 = plan[0, me]
    _, _, am, bm = lax.fori_loop(0, n // 2, walk, (me, b0, me, b0))
    plain = am < bm

    matrix[...] = plane_matrix()
    edge = jnp.zeros((2, CHUNK, 128), jnp.float32)
    for buf in (y0, y1, fil):
        buf[0:2] = edge
        buf[nx + 2 : nx + 4] = edge

    def lap(buf, start, split):
        v = buf[pl.ds(start, BLOCK + 4)]
        mid = v[2 : 2 + BLOCK].reshape(BLOCK * CHUNK, 128)
        high = mid.astype(jnp.bfloat16)
        m = matrix[...]
        out = jnp.dot(high, m, preferred_element_type=jnp.float32)
        if split:
            low = (mid - high.astype(jnp.float32)).astype(jnp.bfloat16)
            out = out + jnp.dot(low, m, preferred_element_type=jnp.float32)
        out = out.reshape(BLOCK, CHUNK, 128)
        out = out + 16.0 * (v[1 : 1 + BLOCK] + v[3 : 3 + BLOCK])
        out = out - (v[0:BLOCK] + v[4 : 4 + BLOCK])
        return v[2 : 2 + BLOCK], out * (1.0 / 24.0)

    def local_pot(start):
        return pot[pl.ds(start, BLOCK), :].reshape(BLOCK, 1, 128)

    blocks = nx // BLOCK

    def each_block(fn):
        if blocks <= 4:
            for b in range(blocks):
                fn(b * BLOCK)
        else:
            def step(b, c):
                fn(pl.multiple_of(b * BLOCK, BLOCK))
                return c

            lax.fori_loop(0, blocks, step, 0)

    def one_chunk(ch, c):
        base = pl.multiple_of(ch * CHUNK, CHUNK)
        wide[...] = orb[pl.ds(base, CHUNK)].astype(jnp.float32).reshape(CHUNK * nx, 128)

        def take(start):
            for j in range(BLOCK):
                y0[start + 2 + j] = wide[pl.ds(start + j, CHUNK, stride=nx), :]

        each_block(take)

        def first(start):
            v, l = lap(y0, start, False)
            y1[pl.ds(start + 2, BLOCK)] = first_scale * ((local_pot(start) - middle_point) * v - l)

        each_block(first)

        def second(start):
            v, l = lap(y1, start, True)
            f = second_scale * ((local_pot(start) - middle_point) * v - l) - back_scale * y0[
                pl.ds(start + 2, BLOCK)
            ]
            f = f.astype(jnp.bfloat16).astype(jnp.float32)
            fil[pl.ds(start + 2, BLOCK)] = f
            for j in range(BLOCK):
                wide[pl.ds(start + j, CHUNK, stride=nx), :] = f[j]

        each_block(second)
        filt[pl.ds(base, CHUNK)] = wide[...].reshape(CHUNK, nx, 128).astype(jnp.bfloat16)

        def third(start):
            v, l = lap(fil, start, False)
            x = jnp.where(plain, v, local_pot(start) * v - l).astype(jnp.bfloat16)
            for q in range(BLOCK // planes):
                for j in range(planes):
                    send[
                        start // planes + q, pl.ds(base, CHUNK), j * 128 : (j + 1) * 128
                    ] = x[q * planes + j]

        each_block(third)

        return c

    lax.fori_loop(0, chunks, one_chunk, 0)
    pl.semaphore_wait(barrier, n - 1)

    def push(o, c):
        d = lax.rem(me + o, n)
        pltpu.make_async_remote_copy(
            src_ref=send.at[d],
            dst_ref=recv.at[lax.rem(d, 2), me],
            send_sem=send_sem,
            recv_sem=recv_sem.at[me],
            device_id={"band": d},
        ).start()
        return c

    lax.fori_loop(1, n, push, 0)
    recv[core, me] = send[me]

    for r in range(ROUNDS):
        def find(j, c, r=r):
            d = 2 * j + core

            def look(i, found):
                return jnp.where(owners[r, i] == d, i, found)

            inverse[r, j] = lax.fori_loop(0, n, look, jnp.int32(0), unroll=8)
            return c

        lax.fori_loop(0, chips, find, 0)

    def relay(source):
        return pltpu.make_async_remote_copy(
            src_ref=recv.at[core, source],
            dst_ref=recv.at[core, source],
            send_sem=relay_send,
            recv_sem=relay_recv,
            device_id={"band": other},
        )

    def pass_on(o, c):
        source = lax.rem(me + n - o, n)
        pltpu.make_async_remote_copy(
            src_ref=send.at[0],
            dst_ref=recv.at[core, source],
            send_sem=send_sem,
            recv_sem=recv_sem.at[source],
            device_id={"band": other},
        ).wait_recv()
        relay(source).start()
        return c

    relay(me).start()
    lax.fori_loop(1, n, pass_on, 0)
    relayed = pltpu.make_async_remote_copy(
        src_ref=recv.at[core],
        dst_ref=recv.at[1 - core],
        send_sem=relay_send,
        recv_sem=relay_recv,
        device_id={"band": other},
    )
    relayed.wait_recv()

    lead = 128 - bands
    tail = bands - lead
    strips = -(-bands // tail)
    lanes = lax.broadcasted_iota(jnp.int32, (bands, 128), 1)
    tail_lanes = lax.broadcasted_iota(jnp.int32, (tail, 128), 1)

    def product(r, j):
        i = inverse[r, j]
        p = plan[r, i]
        blank = jnp.zeros((lead, planes * 128), jnp.bfloat16)
        total = None
        for half in range(2):
            left = recv[half, i]
            right = recv[half, p]
            if r == 0:
                right = jnp.concatenate([right, blank], axis=0)
            else:
                right = jnp.concatenate([right[lead:], blank, right[:lead]], axis=0)
            term = lax.dot_general(
                left, right, (((1,), (1,)), ((), ())), preferred_element_type=jnp.float32
            )
            total = term if total is None else total + term
        return total * norm

    def packed(j):
        one, two = product(0, j), product(1, j)
        top = jnp.where(lanes < bands, one, two)
        low = jnp.zeros((tail, 128), jnp.float32)
        for q in range(strips):
            rows = two[q * tail : min(bands, (q + 1) * tail)]
            if rows.shape[0] < tail:
                rows = jnp.concatenate(
                    [rows, jnp.zeros((tail - rows.shape[0], 128), jnp.float32)], axis=0
                )
            if q > 0:
                rows = pltpu.roll(rows, q * tail, 1)
            here = (tail_lanes >= q * tail) & (tail_lanes < (q + 1) * tail)
            low = jnp.where(here, rows, low)
        return top, low

    def produce(o, c):
        j = lax.rem(chip + o, chips)
        top, low = packed(j)
        part[j, 0:bands] = top.astype(jnp.bfloat16)
        part[j, bands : bands + tail] = low.astype(jnp.bfloat16)
        pltpu.make_async_remote_copy(
            src_ref=part.at[j],
            dst_ref=gathered.at[chip],
            send_sem=part_send,
            recv_sem=part_recv,
            device_id={"band": 2 * j + core},
        ).start()
        return c

    lax.fori_loop(chips // 2, chips, produce, 0)
    lax.fori_loop(1, chips // 2, produce, 0)
    top, low = packed(chip)
    gathered[chip] = jnp.zeros((bands + tail, 128), jnp.bfloat16)
    last = pltpu.make_async_remote_copy(
        src_ref=part.at[0 : chips - 1],
        dst_ref=gathered.at[0 : chips - 1],
        send_sem=part_send,
        recv_sem=part_recv,
        device_id={"band": other},
    )
    last.wait_recv()
    if chips <= 8:
        for s in range(chips):
            top = top + gathered[s, 0:bands].astype(jnp.float32)
            low = low + gathered[s, bands : bands + tail].astype(jnp.float32)
    else:
        def add(s, c):
            return (
                c[0] + gathered[s, 0:bands].astype(jnp.float32),
                c[1] + gathered[s, bands : bands + tail].astype(jnp.float32),
            )

        top, low = lax.fori_loop(0, chips, add, (top, low))
    tiles[0] = top[:, 0:bands]
    front = pltpu.roll(top, lead, 1)
    backs = []
    for q in range(strips):
        rows = pltpu.roll(low, (lead - q * tail) % 128, 1) if lead != q * tail else low
        backs.append(rows[0 : min(tail, bands - q * tail)])
    back = jnp.concatenate(backs, axis=0)
    tiles[1] = jnp.where(lanes < lead, front, back)[:, 0:bands]

    last.wait_send()
    relayed.wait_send()
    pltpu.make_async_remote_copy(
        src_ref=send.at[0 : n - 1],
        dst_ref=recv.at[core, 0 : n - 1],
        send_sem=send_sem,
        recv_sem=recv_sem.at[me],
        device_id={"band": other},
    ).wait_send()


def on_device(orbitals, potential, plan, owners):
    n = lax.axis_size("band")
    bands, nx, cells = orbitals.shape
    planes = nx // n
    vmem = pl.BlockSpec(memory_space=pltpu.VMEM)
    smem = pl.BlockSpec(memory_space=pltpu.SMEM)
    dma = pltpu.SemaphoreType.DMA
    shapes = [((bands, nx, cells), jnp.bfloat16), ((ROUNDS, bands, bands), jnp.float32)]
    return tuple(pl.pallas_call(
        functools.partial(body, n),
        out_shape=[pltpu.VMEM(shape, dtype) for shape, dtype in shapes],
        in_specs=[vmem, vmem, smem, smem],
        out_specs=[vmem, vmem],
        scratch_shapes=[
            pltpu.VMEM((CHUNK * nx, 128), jnp.float32),
            pltpu.VMEM((nx + 4, CHUNK, 128), jnp.float32),
            pltpu.VMEM((nx + 4, CHUNK, 128), jnp.float32),
            pltpu.VMEM((nx + 4, CHUNK, 128), jnp.float32),
            pltpu.VMEM((128, 128), jnp.bfloat16),
            pltpu.VMEM((n, bands, planes * 128), jnp.bfloat16),
            pltpu.VMEM((2, n, bands, planes * 128), jnp.bfloat16),
            pltpu.VMEM((n // 2, 2 * bands - (128 - bands), 128), jnp.bfloat16),
            pltpu.VMEM((n // 2, 2 * bands - (128 - bands), 128), jnp.bfloat16),
            pltpu.SMEM((ROUNDS, n // 2), jnp.int32),
            dma,
            dma((n,)),
            dma,
            dma,
            dma,
            dma,
        ],
        compiler_params=pltpu.CompilerParams(
            collective_id=0, has_side_effects=True, vmem_limit_bytes=48 * 2**20
        ),
    )(orbitals, potential, plan, owners))


def solution(mesh):
    placed = (
        P(("groups", "band"), None, None),
        P("groups", None),
        P("groups", None),
        P("groups", None),
    )
    return jax.shard_map(
        on_device,
        mesh=mesh,
        in_specs=placed,
        out_specs=(P(("groups", "band"), None, None), P(None, ("groups", "band"), None)),
        check_vma=False,
    )
```

```python
import functools
import math

import jax
import jax.numpy as jnp
from jax import lax
from jax.experimental import pallas as pl
from jax.experimental.pallas import tpu as pltpu
from jax.sharding import PartitionSpec as P

NZ = 16
ROUNDS = 2
CHUNK = 16
BLOCK = 8
VMEM_BYTES = 67043328
SPARE_BYTES = 4096

lower_edge = -2.5
cutoff_edge = 4.0
upper_edge = 8.5
half_width = (upper_edge - cutoff_edge) / 2.0
middle_point = (upper_edge + cutoff_edge) / 2.0
sigma_zero = half_width / (lower_edge - middle_point)
sigma_next = 1.0 / (2.0 / sigma_zero - sigma_zero)
first_scale = sigma_zero / half_width
second_scale = 2.0 * sigma_next / half_width
back_scale = sigma_zero * sigma_next


def plane_matrix():
    row = lax.broadcasted_iota(jnp.int32, (128, 128), 0)
    col = lax.broadcasted_iota(jnp.int32, (128, 128), 1)
    gap = jnp.abs(row - col)
    same = (row // NZ) == (col // NZ)
    near = (same & (gap == 1)) | (gap == NZ)
    far = (same & (gap == 2)) | (gap == 2 * NZ)
    return jnp.where(
        gap == 0, -90.0, jnp.where(near, 16.0, jnp.where(far, -1.0, 0.0))
    ).astype(jnp.bfloat16)


def body(
    n, orb_in, pot_in, plan_in, owners_in, filt, tiles,
    orb, pot, plan, owners, load_sem,
    wide, y0, y1, fil, matrix, send, recv, part, gathered, inverse,
    send_sem, recv_sem, relay_send, relay_recv, part_send, part_recv,
):
    loads = [
        pltpu.make_async_copy(a, b, load_sem.at[k])
        for k, (a, b) in enumerate(
            ((plan_in, plan), (owners_in, owners), (orb_in, orb), (pot_in, pot))
        )
    ]
    for load in loads:
        load.start()

    me = lax.axis_index("band")
    core = lax.rem(me, 2)
    chip = me // 2
    chips = n // 2
    other = me + 1 - 2 * core
    bands, nx = orb.shape[0], orb.shape[1]
    chunks = bands // CHUNK
    planes = nx // n
    norm = 1.0 / math.sqrt(nx * orb.shape[2])

    barrier = pltpu.get_barrier_semaphore()

    def greet(o, c):
        pl.semaphore_signal(barrier, inc=1, device_id={"band": lax.rem(me + o, n)})
        return c

    lax.fori_loop(1, n, greet, 0)
    for load in loads:
        load.wait()

    def walk(_, c):
        a, b, am, bm = c
        a = plan[1, plan[0, a]]
        b = plan[1, plan[0, b]]
        return a, b, jnp.minimum(am, a), jnp.minimum(bm, b)

    b0 = plan[0, me]
    _, _, am, bm = lax.fori_loop(0, n // 2, walk, (me, b0, me, b0))
    plain = am < bm

    matrix[...] = plane_matrix()
    edge = jnp.zeros((2, CHUNK, 128), jnp.float32)
    for buf in (y0, y1, fil):
        buf[0:2] = edge
        buf[nx + 2 : nx + 4] = edge

    def lap(buf, start, split):
        v = buf[pl.ds(start, BLOCK + 4)]
        mid = v[2 : 2 + BLOCK].reshape(BLOCK * CHUNK, 128)
        high = mid.astype(jnp.bfloat16)
        m = matrix[...]
        out = jnp.dot(high, m, preferred_element_type=jnp.float32)
        if split:
            low = (mid - high.astype(jnp.float32)).astype(jnp.bfloat16)
            out = out + jnp.dot(low, m, preferred_element_type=jnp.float32)
        out = out.reshape(BLOCK, CHUNK, 128)
        out = out + 16.0 * (v[1 : 1 + BLOCK] + v[3 : 3 + BLOCK])
        out = out - (v[0:BLOCK] + v[4 : 4 + BLOCK])
        return v[2 : 2 + BLOCK], out * (1.0 / 24.0)

    def local_pot(start):
        return pot[pl.ds(start, BLOCK), :].reshape(BLOCK, 1, 128)

    blocks = nx // BLOCK

    def each_block(fn):
        if blocks <= 4:
            for b in range(blocks):
                fn(b * BLOCK)
        else:
            def step(b, c):
                fn(pl.multiple_of(b * BLOCK, BLOCK))
                return c

            lax.fori_loop(0, blocks, step, 0)

    def one_chunk(ch, c):
        base = pl.multiple_of(ch * CHUNK, CHUNK)
        wide[...] = orb[pl.ds(base, CHUNK)].astype(jnp.float32).reshape(CHUNK * nx, 128)

        def take(start):
            for j in range(BLOCK):
                y0[start + 2 + j] = wide[pl.ds(start + j, CHUNK, stride=nx), :]

        each_block(take)

        def first(start):
            v, l = lap(y0, start, False)
            y1[pl.ds(start + 2, BLOCK)] = first_scale * ((local_pot(start) - middle_point) * v - l)

        each_block(first)

        def second(start):
            v, l = lap(y1, start, True)
            f = second_scale * ((local_pot(start) - middle_point) * v - l) - back_scale * y0[
                pl.ds(start + 2, BLOCK)
            ]
            f = f.astype(jnp.bfloat16).astype(jnp.float32)
            fil[pl.ds(start + 2, BLOCK)] = f
            for j in range(BLOCK):
                wide[pl.ds(start + j, CHUNK, stride=nx), :] = f[j]

        each_block(second)
        filt[pl.ds(base, CHUNK)] = wide[...].reshape(CHUNK, nx, 128).astype(jnp.bfloat16)

        def third(start):
            v, l = lap(fil, start, False)
            x = jnp.where(plain, v, local_pot(start) * v - l).astype(jnp.bfloat16)
            for q in range(BLOCK // planes):
                for j in range(planes):
                    send[
                        start // planes + q, pl.ds(base, CHUNK), j * 128 : (j + 1) * 128
                    ] = x[q * planes + j]

        each_block(third)

        return c

    lax.fori_loop(0, chunks, one_chunk, 0)
    pl.semaphore_wait(barrier, n - 1)

    def push(o, c):
        d = lax.rem(me + o, n)
        pltpu.make_async_remote_copy(
            src_ref=send.at[d],
            dst_ref=recv.at[lax.rem(d, 2), me],
            send_sem=send_sem,
            recv_sem=recv_sem.at[me],
            device_id={"band": d},
        ).start()
        return c

    lax.fori_loop(1, n, push, 0)
    recv[core, me] = send[me]

    for r in range(ROUNDS):
        def find(j, c, r=r):
            d = 2 * j + core

            def look(i, found):
                return jnp.where(owners[r, i] == d, i, found)

            inverse[r, j] = lax.fori_loop(0, n, look, jnp.int32(0), unroll=8)
            return c

        lax.fori_loop(0, chips, find, 0)

    def relay(source):
        return pltpu.make_async_remote_copy(
            src_ref=recv.at[core, source],
            dst_ref=recv.at[core, source],
            send_sem=relay_send,
            recv_sem=relay_recv,
            device_id={"band": other},
        )

    def pass_on(o, c):
        source = lax.rem(me + n - o, n)
        pltpu.make_async_remote_copy(
            src_ref=send.at[0],
            dst_ref=recv.at[core, source],
            send_sem=send_sem,
            recv_sem=recv_sem.at[source],
            device_id={"band": other},
        ).wait_recv()
        relay(source).start()
        return c

    relay(me).start()
    lax.fori_loop(1, n, pass_on, 0)
    relayed = pltpu.make_async_remote_copy(
        src_ref=recv.at[core],
        dst_ref=recv.at[1 - core],
        send_sem=relay_send,
        recv_sem=relay_recv,
        device_id={"band": other},
    )
    relayed.wait_recv()

    lead = 128 - bands
    tail = bands - lead
    strips = -(-bands // tail)
    lanes = lax.broadcasted_iota(jnp.int32, (bands, 128), 1)
    tail_lanes = lax.broadcasted_iota(jnp.int32, (tail, 128), 1)

    def product(r, j):
        i = inverse[r, j]
        p = plan[r, i]
        blank = jnp.zeros((lead, planes * 128), jnp.bfloat16)
        total = None
        for half in range(2):
            left = recv[half, i]
            right = recv[half, p]
            if r == 0:
                right = jnp.concatenate([right, blank], axis=0)
            else:
                right = jnp.concatenate([right[lead:], blank, right[:lead]], axis=0)
            term = lax.dot_general(
                left, right, (((1,), (1,)), ((), ())), preferred_element_type=jnp.float32
            )
            total = term if total is None else total + term
        return total * norm

    def packed(j):
        one, two = product(0, j), product(1, j)
        top = jnp.where(lanes < bands, one, two)
        low = jnp.zeros((tail, 128), jnp.float32)
        for q in range(strips):
            rows = two[q * tail : min(bands, (q + 1) * tail)]
            if rows.shape[0] < tail:
                rows = jnp.concatenate(
                    [rows, jnp.zeros((tail - rows.shape[0], 128), jnp.float32)], axis=0
                )
            if q > 0:
                rows = pltpu.roll(rows, q * tail, 1)
            here = (tail_lanes >= q * tail) & (tail_lanes < (q + 1) * tail)
            low = jnp.where(here, rows, low)
        return top, low

    def produce(o, c):
        j = lax.rem(chip + o, chips)
        top, low = packed(j)
        part[j, 0:bands] = top.astype(jnp.bfloat16)
        part[j, bands : bands + tail] = low.astype(jnp.bfloat16)
        pltpu.make_async_remote_copy(
            src_ref=part.at[j],
            dst_ref=gathered.at[chip],
            send_sem=part_send,
            recv_sem=part_recv,
            device_id={"band": 2 * j + core},
        ).start()
        return c

    lax.fori_loop(chips // 2, chips, produce, 0)
    lax.fori_loop(1, chips // 2, produce, 0)
    top, low = packed(chip)
    gathered[chip] = jnp.zeros((bands + tail, 128), jnp.bfloat16)
    last = pltpu.make_async_remote_copy(
        src_ref=part.at[0 : chips - 1],
        dst_ref=gathered.at[0 : chips - 1],
        send_sem=part_send,
        recv_sem=part_recv,
        device_id={"band": other},
    )
    last.wait_recv()
    if chips <= 8:
        for s in range(chips):
            top = top + gathered[s, 0:bands].astype(jnp.float32)
            low = low + gathered[s, bands : bands + tail].astype(jnp.float32)
    else:
        def add(s, c):
            return (
                c[0] + gathered[s, 0:bands].astype(jnp.float32),
                c[1] + gathered[s, bands : bands + tail].astype(jnp.float32),
            )

        top, low = lax.fori_loop(0, chips, add, (top, low))
    tiles[0] = top[:, 0:bands]
    front = pltpu.roll(top, lead, 1)
    backs = []
    for q in range(strips):
        rows = pltpu.roll(low, (lead - q * tail) % 128, 1) if lead != q * tail else low
        backs.append(rows[0 : min(tail, bands - q * tail)])
    back = jnp.concatenate(backs, axis=0)
    tiles[1] = jnp.where(lanes < lead, front, back)[:, 0:bands]

    last.wait_send()
    relayed.wait_send()
    pltpu.make_async_remote_copy(
        src_ref=send.at[0 : n - 1],
        dst_ref=recv.at[core, 0 : n - 1],
        send_sem=send_sem,
        recv_sem=recv_sem.at[me],
        device_id={"band": other},
    ).wait_send()


def write_out(filt, tiles, filt_out, tiles_out, sem):
    copies = [
        pltpu.make_async_copy(filt, filt_out, sem.at[0]),
        pltpu.make_async_copy(tiles, tiles_out, sem.at[1]),
    ]
    for copy in copies:
        copy.start()
    for copy in copies:
        copy.wait()


def on_device(orbitals, potential, plan, owners):
    n = lax.axis_size("band")
    bands, nx, cells = orbitals.shape
    planes = nx // n
    vmem = pl.BlockSpec(memory_space=pltpu.VMEM)
    dma = pltpu.SemaphoreType.DMA
    shapes = [((bands, nx, cells), jnp.bfloat16), ((ROUNDS, bands, bands), jnp.float32)]
    held_bytes = bands * nx * cells * 2 + ROUNDS * bands * 128 * 4
    held = pl.pallas_call(
        functools.partial(body, n),
        out_shape=[pltpu.VMEM(shape, dtype) for shape, dtype in shapes],
        in_specs=[pl.BlockSpec(memory_space=pltpu.HBM)] * 4,
        out_specs=[vmem, vmem],
        scratch_shapes=[
            pltpu.VMEM((bands, nx, cells), jnp.bfloat16),
            pltpu.VMEM((nx, cells), jnp.float32),
            pltpu.SMEM(plan.shape, jnp.int32),
            pltpu.SMEM(owners.shape, jnp.int32),
            dma((4,)),
            pltpu.VMEM((CHUNK * nx, 128), jnp.float32),
            pltpu.VMEM((nx + 4, CHUNK, 128), jnp.float32),
            pltpu.VMEM((nx + 4, CHUNK, 128), jnp.float32),
            pltpu.VMEM((nx + 4, CHUNK, 128), jnp.float32),
            pltpu.VMEM((128, 128), jnp.bfloat16),
            pltpu.VMEM((n, bands, planes * 128), jnp.bfloat16),
            pltpu.VMEM((2, n, bands, planes * 128), jnp.bfloat16),
            pltpu.VMEM((n // 2, 2 * bands - (128 - bands), 128), jnp.bfloat16),
            pltpu.VMEM((n // 2, 2 * bands - (128 - bands), 128), jnp.bfloat16),
            pltpu.SMEM((ROUNDS, n // 2), jnp.int32),
            dma,
            dma((n,)),
            dma,
            dma,
            dma,
            dma,
        ],
        compiler_params=pltpu.CompilerParams(
            collective_id=0, has_side_effects=True, vmem_limit_bytes=VMEM_BYTES - held_bytes - SPARE_BYTES
        ),
    )(orbitals, potential, plan, owners)
    return pl.pallas_call(
        write_out,
        out_shape=[jax.ShapeDtypeStruct(shape, dtype) for shape, dtype in shapes],
        in_specs=[pl.BlockSpec(memory_space=pl.ANY)] * 2,
        out_specs=[pl.BlockSpec(memory_space=pl.ANY)] * 2,
        scratch_shapes=[dma((2,))],
        compiler_params=pltpu.CompilerParams(vmem_limit_bytes=2**20),
    )(*held)


def solution(mesh):
    placed = (
        P(("groups", "band"), None, None),
        P("groups", None),
        P("groups", None),
        P("groups", None),
    )
    return jax.shard_map(
        on_device,
        mesh=mesh,
        in_specs=placed,
        out_specs=(P(("groups", "band"), None, None), P(None, ("groups", "band"), None)),
        check_vma=False,
    )
```
